256 devices in a mesh: outer: 32 (over z, x), inner: 8 (over y, core).
Axes of the slice: x: 4, y: 4, z: 8, core: 2. Of those that a mesh axis runs over, the one named last changes fastest.
Arguments:
- queries: bfloat16 [32768, 2048], P(('outer', 'inner')), may hold values from -5 to 5
- key_rows: bfloat16 [32768, 2048], P(('outer', 'inner')), may hold values from -5 to 5
- value_rows: bfloat16 [32768, 2048], P(('outer', 'inner')), may hold values from -6 to 6
- out_grad: bfloat16 [32768, 2048], P(('outer', 'inner')), may hold values from -6 to 6
- log_gate: float32 [16, 32768], P(None, ('outer', 'inner')), may hold values from -1 to 0
Outputs:
- mixed_out: bfloat16 [32768, 2048], P(('outer', 'inner'))
- query_grad: bfloat16 [32768, 2048], P(('outer', 'inner'))
- key_grad: bfloat16 [32768, 2048], P(('outer', 'inner'))
- value_grad: bfloat16 [32768, 2048], P(('outer', 'inner'))
The draws below stay inside these ranges and needn't reach their ends.
All inputs are finite; a program needn't handle non-finite values.
Results may differ from the reference program's by a relative error of at most 0.007.
Values may be sent and summed in bfloat16 or wider, within the bound.
No kernel may reach another device: no remote copies, remote signals or barrier semaphores. Data moves between devices by JAX's collectives and lax.ppermute only.
A program may use at most 256 MiB of HBM per device.

```python
import math
import jax
import jax.numpy as jnp
from jax import lax

H = 16
DH = 128
W = 64
TOK_DEV = 128
D = 2048
SEQUENCE_TOKENS = 32768


def rows_pair(key):
    root_random_key = jax.random.fold_in(key, 4242)
    query_key, rows_key = jax.random.split(root_random_key, 2)
    shape_all = (SEQUENCE_TOKENS, H * DH)
    query_part = jnp.clip(jax.random.normal(query_key, shape_all, jnp.float32), -4.0, 4.0)
    key_part = jnp.clip(jax.random.normal(rows_key, shape_all, jnp.float32), -4.0, 4.0)
    return (query_part, key_part)


def draw_queries(key, part):
    return rows_pair(key)[0].astype(jnp.bfloat16)


def draw_key_rows(key, part):
    return rows_pair(key)[1].astype(jnp.bfloat16)


def draw_log_gate(key, part):
    root_random_key = jax.random.fold_in(key, 77)
    variant_random_key, quick_random_key, gradual_random_key, token_random_key, block_random_key, spike_random_key, depth_random_key = jax.random.split(root_random_key, 7)
    chance = 0.5
    slow_heads = jax.random.uniform(variant_random_key, (H, 1), jnp.float32) < chance
    fast_rate = jnp.exp(jax.random.uniform(quick_random_key, (H, 1), jnp.float32, math.log(1.0 / 50.0), math.log(1.0 / 30.0)))
    slow_rate = (0.1 + 0.2 * jax.random.uniform(gradual_random_key, (H, 1), jnp.float32)) / SEQUENCE_TOKENS
    head_decay_rate = jnp.where(slow_heads, slow_rate, fast_rate)
    token_multiplier = jax.random.uniform(token_random_key, (H, SEQUENCE_TOKENS), jnp.float32, 0.5, 1.5)
    block_multiplier = jax.random.uniform(block_random_key, (H, SEQUENCE_TOKENS // TOK_DEV, 1), jnp.float32, 0.5, 1.5)
    block_multiplier = jnp.broadcast_to(block_multiplier, (H, SEQUENCE_TOKENS // TOK_DEV, TOK_DEV)).reshape(H, SEQUENCE_TOKENS)
    device_layout = jax.random.randint(spike_random_key, (3,), 0, SEQUENCE_TOKENS)
    spike_present = jnp.any(jnp.arange(SEQUENCE_TOKENS)[None, :] == device_layout[:, None], axis=0)
    spike_depth = jnp.log(jax.random.uniform(depth_random_key, (1, SEQUENCE_TOKENS), jnp.float32, 0.6, 0.8))
    gate_logarithm = -head_decay_rate * token_multiplier * block_multiplier + jnp.where(spike_present[None, :], spike_depth, 0.0)
    return gate_logarithm.astype(jnp.float32)


def block_levels(rng, shape, cuts, smallest, largest):
    level = 1.0
    for position, parts in cuts:
        steps = jax.random.uniform(jax.random.fold_in(jax.random.fold_in(rng, 6), position), (parts,), jnp.float32, smallest / len(cuts), largest / len(cuts))
        level = level * jnp.repeat(jnp.exp(steps), shape[position] // parts).reshape((-1,) + (1,) * (len(shape) - 1 - position))
    return level


def gaussian(key, shape, width, most, pieces=(), kind=jnp.bfloat16):
    array = width * jax.random.normal(key, shape, jnp.float32)
    if pieces:
        array = array * block_levels(key, shape, pieces, -0.22, 0.18)
    return jnp.clip(array, -most, most).astype(kind)


def setup_inputs(seed: int = 0) -> dict:
    key_list = jax.random.split(jax.random.key(seed), 6)
    queries = draw_queries(jax.random.fold_in(key_list[5], 71), 0)
    key_rows = draw_key_rows(jax.random.fold_in(key_list[5], 71), 0)
    value_rows = gaussian(key_list[2], (SEQUENCE_TOKENS, D), 1.0, 6.0, ((0, 256),))
    out_grad = gaussian(key_list[3], (SEQUENCE_TOKENS, D), 1.0, 6.0, ((0, 256),))
    log_gate = draw_log_gate(jax.random.fold_in(key_list[5], 71), 0)
    return dict(queries=queries, key_rows=key_rows, value_rows=value_rows, out_grad=out_grad, log_gate=log_gate)


def product(form, left, right):
    return jnp.einsum(form, left.astype(jnp.float32), right.astype(jnp.float32), precision=lax.Precision.HIGHEST)


def local_states(query_blk, key_blk, value_blk, grad_blk, gate_rows):
    cumul_gate = jnp.cumsum(gate_rows, axis=1)
    last_cumul = cumul_gate[:, -1:]
    block_decay = jnp.exp(cumul_gate[:, -1])
    tail_weight = jnp.exp(last_cumul - cumul_gate).T
    head_weight = jnp.exp(cumul_gate).T
    state_local = product("thf,the->hfe", key_blk.astype(jnp.float32) * tail_weight[:, :, None], value_blk)
    grad_local = product("thf,the->hfe", query_blk.astype(jnp.float32) * head_weight[:, :, None], grad_blk)
    return block_decay, state_local, grad_local


def block_terms(query_blk, key_blk, value_blk, grad_blk, gate_rows, state_in, grad_after, key_halo, value_halo, halo_live, lin_scale):
    row_count = query_blk.shape[0]
    halo_rows = key_halo.shape[0]
    head_size = query_blk.shape[2]
    cumul_gate = jnp.cumsum(gate_rows, axis=1)
    last_cumul = cumul_gate[:, -1:]
    head_weight = jnp.exp(cumul_gate).T
    tail_weight = jnp.exp(last_cumul - cumul_gate).T
    query_pos = jnp.arange(row_count)[:, None]
    key_pos = jnp.arange(row_count)[None, :]
    causal_mask = (key_pos <= query_pos)[None]
    gap_logs = cumul_gate[:, :, None] - cumul_gate[:, None, :]
    decay_grid = jnp.where(causal_mask, jnp.exp(jnp.where(causal_mask, gap_logs, 0.0)), 0.0)
    lin_weight = (product("thf,shf->hts", query_blk, key_blk) * decay_grid).astype(jnp.bfloat16)
    query_decayed = query_blk.astype(jnp.float32) * head_weight[:, :, None]
    lin_out = product("hts,she->the", lin_weight, value_blk) + product("thf,hfe->the", query_decayed, state_in)
    ext_keys = jnp.concatenate([key_halo, key_blk], axis=0)
    ext_values = jnp.concatenate([value_halo, value_blk], axis=0)
    ext_pos = jnp.arange(row_count + halo_rows)[None, :]
    in_band = ((ext_pos > query_pos) & (ext_pos <= query_pos + halo_rows) & ((ext_pos >= halo_rows) | halo_live))[None]
    logits = product("thf,jhf->htj", query_blk, ext_keys) * head_size ** -0.5
    masked_logits = jnp.where(in_band, logits, -jnp.inf)
    row_max = jnp.max(masked_logits, axis=2, keepdims=True)
    expo_terms = jnp.exp(masked_logits - row_max)
    win_prob = expo_terms / jnp.sum(expo_terms, axis=2, keepdims=True)
    prob_low = win_prob.astype(jnp.bfloat16)
    win_out = product("htj,jhe->the", prob_low, ext_values)
    output = (lin_scale * lin_out + win_out).astype(jnp.bfloat16)
    grad_weight = (product("the,she->hts", grad_blk, value_blk) * decay_grid).astype(jnp.bfloat16)
    grad_decayed = grad_blk.astype(jnp.float32) * head_weight[:, :, None]
    query_lin = product("hts,shf->thf", grad_weight, key_blk) + product("the,hfe->thf", grad_decayed, state_in)
    value_tail = value_blk.astype(jnp.float32) * tail_weight[:, :, None]
    key_tail = key_blk.astype(jnp.float32) * tail_weight[:, :, None]
    key_lin = product("hts,thf->shf", grad_weight, query_blk) + product("she,hfe->shf", value_tail, grad_after)
    value_lin = product("hts,the->she", lin_weight, grad_blk) + product("shf,hfe->she", key_tail, grad_after)
    prob_grad = product("the,jhe->htj", grad_blk, ext_values)
    row_delta = jnp.sum(win_prob * prob_grad, axis=2, keepdims=True)
    logit_grad = (win_prob * (prob_grad - row_delta) * head_size ** -0.5).astype(jnp.bfloat16)
    query_win = product("htj,jhf->thf", logit_grad, ext_keys)
    key_ext = product("htj,thf->jhf", logit_grad, query_blk)
    value_ext = product("htj,the->jhe", prob_low, grad_blk)
    query_grad = (lin_scale * query_lin + query_win).astype(jnp.bfloat16)
    key_local = lin_scale * key_lin + key_ext[halo_rows:]
    value_local = lin_scale * value_lin + value_ext[halo_rows:]
    return output, query_grad, key_local, value_local, key_ext[:halo_rows], value_ext[:halo_rows]


def reference(queries, key_rows, value_rows, out_grad, log_gate):
    blocks = SEQUENCE_TOKENS // TOK_DEV
    block_shape = (blocks, TOK_DEV, H, DH)
    query_blocks = queries.reshape(block_shape)
    key_blocks = key_rows.reshape(block_shape)
    value_blocks = value_rows.reshape(block_shape)
    grad_blocks = out_grad.reshape(block_shape)
    gate_blocks = log_gate.reshape(H, blocks, TOK_DEV).transpose(1, 0, 2)
    lin_scale = (DH * SEQUENCE_TOKENS) ** -0.5

    def local_step(elements):
        return local_states(*elements)

    decays, states, grad_states = lax.map(local_step, (query_blocks, key_blocks, value_blocks, grad_blocks, gate_blocks))

    def back_step(running, elements):
        block_decay, grad_local = elements
        return grad_local + block_decay[:, None, None] * running, running

    zero_state = jnp.zeros((H, DH, DH), jnp.float32)
    final_back, grad_after = lax.scan(back_step, zero_state, (decays, grad_states), reverse=True)

    def forward_step(running, elements):
        state_in, key_halo, value_halo, key_pending, value_pending = running
        block_pos, query_blk, key_blk, value_blk, grad_blk, gate_rows, block_decay, state_local, grad_out = elements
        output, query_grad, key_local, value_local, key_back, value_back = block_terms(
            query_blk, key_blk, value_blk, grad_blk, gate_rows, state_in, grad_out, key_halo, value_halo, block_pos > 0, lin_scale)
        key_done = key_pending.at[-W:].add(key_back).astype(jnp.bfloat16)
        value_done = value_pending.at[-W:].add(value_back).astype(jnp.bfloat16)
        state_next = block_decay[:, None, None] * state_in + state_local
        return (state_next, key_blk[-W:], value_blk[-W:], key_local, value_local), (output, query_grad, key_done, value_done)

    start = (zero_state, jnp.zeros((W, H, DH), jnp.bfloat16), jnp.zeros((W, H, DH), jnp.bfloat16),
             jnp.zeros((TOK_DEV, H, DH), jnp.float32), jnp.zeros((TOK_DEV, H, DH), jnp.float32))
    final_carry, stacked = lax.scan(forward_step, start, (jnp.arange(blocks), query_blocks, key_blocks, value_blocks,
                                                          grad_blocks, gate_blocks, decays, states, grad_after))
    outputs, query_grads, key_done, value_done = stacked
    key_grad = jnp.concatenate([key_done[1:], final_carry[3].astype(jnp.bfloat16)[None]], axis=0)
    value_grad = jnp.concatenate([value_done[1:], final_carry[4].astype(jnp.bfloat16)[None]], axis=0)
    return (outputs.reshape(SEQUENCE_TOKENS, H * DH), query_grads.reshape(SEQUENCE_TOKENS, H * DH),
            key_grad.reshape(SEQUENCE_TOKENS, H * DH), value_grad.reshape(SEQUENCE_TOKENS, H * DH))
```

```python
import jax
import jax.numpy as jnp
from jax import lax
from jax.experimental import pallas as pl
from jax.experimental.pallas import tpu as pltpu
from jax.sharding import Mesh
from jax.sharding import PartitionSpec as P

AXES = ("z", "x", "y", "c")
GRID = (8, 4, 4, 2)
PLANE = 16
W = 64
DH = 128
HALF = 8
COLS = HALF * DH
MSG = 144
F32 = jnp.float32
BF16 = jnp.bfloat16


def dot(a, b, ca, cb):
    return lax.dot_general(a, b, (((ca,), (cb,)), ((), ())), preferred_element_type=F32)


def cumulative(gates):
    n = gates.shape[1]
    i = lax.broadcasted_iota(jnp.int32, (n, n), 0)
    j = lax.broadcasted_iota(jnp.int32, (n, n), 1)
    upper = (i <= j).astype(F32)
    rows = lax.dot_general(gates, upper, (((1,), (0,)), ((), ())), precision=lax.Precision.HIGHEST, preferred_element_type=F32)
    return rows, rows.T


def decay_tile(d):
    d = jnp.broadcast_to(d, (16, DH))
    hi = d.astype(BF16).astype(F32)
    mid = (d - hi).astype(BF16).astype(F32)
    low = d - hi - mid
    row = lax.broadcasted_iota(jnp.int32, (16, DH), 0)
    zero = jnp.zeros_like(d)
    return jnp.where(row == 0, hi, jnp.where(row == 1, mid, jnp.where(row == 2, low, zero))).astype(BF16)


def decay_of(tile):
    return jnp.sum(tile.astype(F32), axis=0, keepdims=True)


def states_kernel(sel_ref, q_ref, k_ref, v_ref, g_ref, gate_ref, msg_ref):
    rows, cols = cumulative(gate_ref[...])
    for j in range(HALF):
        at = slice(j * DH, (j + 1) * DH)
        last = rows[j : j + 1, DH - 1 : DH]
        head = jnp.exp(cols[:, j : j + 1])
        tail = jnp.exp(last - cols[:, j : j + 1])
        kt = (k_ref[:, at].astype(F32) * tail).astype(BF16)
        qh = (q_ref[:, at].astype(F32) * head).astype(BF16)
        s = dot(kt, v_ref[:, at], 0, 0).astype(BF16)
        g = dot(qh, g_ref[:, at], 0, 0).astype(BF16)
        d = decay_tile(jnp.exp(last))
        for r in range(2):
            part = slice(r * 64, (r + 1) * 64)
            msg_ref[2 * j + r, 0:64, :] = s[part]
            msg_ref[2 * j + r, 64:128, :] = g[part]
            msg_ref[2 * j + r, 128:144, :] = d


def combine_kernel(c_ref, own_ref, other_ref, out_ref):
    first = c_ref[0] == 0

    def body(a_ref, b_ref):
        for p in range(PLANE):
            da = decay_of(a_ref[p, 128:144, :])
            db = decay_of(b_ref[p, 128:144, :])
            out_ref[p, 0:64, :] = (db * a_ref[p, 0:64, :].astype(F32) + b_ref[p, 0:64, :].astype(F32)).astype(BF16)
            out_ref[p, 64:128, :] = (a_ref[p, 64:128, :].astype(F32) + da * b_ref[p, 64:128, :].astype(F32)).astype(BF16)
            out_ref[p, 128:144, :] = decay_tile(da * db)

    @pl.when(first)
    def _():
        body(own_ref, other_ref)

    @pl.when(jnp.logical_not(first))
    def _():
        body(other_ref, own_ref)


def plane_kernel(msg_ref, out_ref):
    fwd = jnp.zeros((64, DH), F32)
    bwd = jnp.zeros((64, DH), F32)
    d = jnp.ones((1, DH), F32)
    for p in range(PLANE):
        b = PLANE - 1 - p
        dp = decay_of(msg_ref[p, 128:144, :])
        fwd = dp * fwd + msg_ref[p, 0:64, :].astype(F32)
        bwd = decay_of(msg_ref[b, 128:144, :]) * bwd + msg_ref[b, 64:128, :].astype(F32)
        d = d * dp
    tile = decay_tile(d)
    for z in range(GRID[0]):
        out_ref[z, 0:64, :] = fwd.astype(BF16)
        out_ref[z, 64:128, :] = bwd.astype(BF16)
        out_ref[z, 128:144, :] = tile


def incoming_kernel(z_ref, msg_ref, planes_ref, out_ref):
    z = z_ref[0]
    n = GRID[0]
    fwd = jnp.zeros((64, DH), F32)
    bwd = jnp.zeros((64, DH), F32)
    for i in range(n):
        b = n - 1 - i
        new_f = decay_of(planes_ref[i, 128:144, :]) * fwd + planes_ref[i, 0:64, :].astype(F32)
        fwd = jnp.where(i < z, new_f, fwd)
        new_b = decay_of(planes_ref[b, 128:144, :]) * bwd + planes_ref[b, 64:128, :].astype(F32)
        bwd = jnp.where(b > z, new_b, bwd)
    for p in range(PLANE):
        b = PLANE - 1 - p
        out_ref[p, 0:64, :] = fwd.astype(BF16)
        out_ref[b, 64:128, :] = bwd.astype(BF16)
        fwd = decay_of(msg_ref[p, 128:144, :]) * fwd + msg_ref[p, 0:64, :].astype(F32)
        bwd = decay_of(msg_ref[b, 128:144, :]) * bwd + msg_ref[b, 64:128, :].astype(F32)


def hand_kernel(c_ref, chip_ref, own_ref, other_ref, mine_ref, theirs_ref):
    first = c_ref[0] == 0

    def body(is_first):
        for p in range(PLANE):
            fwd = chip_ref[p, 0:64, :]
            bwd = chip_ref[p, 64:128, :]
            inner = own_ref if is_first else other_ref
            outer = other_ref if is_first else own_ref
            late_f = (decay_of(inner[p, 128:144, :]) * fwd.astype(F32) + inner[p, 0:64, :].astype(F32)).astype(BF16)
            early_b = (decay_of(outer[p, 128:144, :]) * bwd.astype(F32) + outer[p, 64:128, :].astype(F32)).astype(BF16)
            early_ref = mine_ref if is_first else theirs_ref
            late_ref = theirs_ref if is_first else mine_ref
            early_ref[p, 0:64, :] = fwd
            early_ref[p, 64:128, :] = early_b
            late_ref[p, 0:64, :] = late_f
            late_ref[p, 64:128, :] = bwd

    @pl.when(first)
    def _():
        body(True)

    @pl.when(jnp.logical_not(first))
    def _():
        body(False)


def window_kernel(lin_scale, live_ref, q_ref, k_ref, v_ref, g_ref, halo_ref, gate_ref, o_ref, qg_ref, kg_ref, vg_ref, back_ref):
    live = live_ref[0] > 0
    rows, cols = cumulative(gate_ref[...])
    t = lax.broadcasted_iota(jnp.int32, (DH, DH), 0)
    lane = lax.broadcasted_iota(jnp.int32, (DH, DH), 1)
    key = jnp.where(t < W, lane - W, lane)
    causal = (key >= 0) & (key <= t)
    banded = (key > t - W) & (key <= t) & ((key >= 0) | live)
    scale = DH**-0.5
    for j in range(HALF):
        at = slice(j * DH, (j + 1) * DH)
        q, k, v, g = q_ref[:, at], k_ref[:, at], v_ref[:, at], g_ref[:, at]
        kx = jnp.concatenate([halo_ref[0:W, at], k[0:W]], axis=0)
        vx = jnp.concatenate([halo_ref[W : 2 * W, at], v[0:W]], axis=0)
        a = jnp.concatenate([dot(q[0:W], kx, 1, 1), dot(q[W:], k, 1, 1)], axis=0)
        b = jnp.concatenate([dot(g[0:W], vx, 1, 1), dot(g[W:], v, 1, 1)], axis=0)
        row = rows[j : j + 1, :]
        shifted = jnp.concatenate([row[:, W:], row[:, :W]], axis=1)
        gap = cols[:, j : j + 1] - jnp.where(t < W, shifted, row)
        decay = jnp.where(causal, jnp.exp(jnp.minimum(gap, 0.0)), 0.0) * lin_scale
        logits = jnp.where(banded, a * scale, -jnp.inf)
        e = jnp.exp(logits - jnp.max(logits, axis=1, keepdims=True))
        prob = e / jnp.sum(e, axis=1, keepdims=True)
        delta = jnp.sum(prob * b, axis=1, keepdims=True)
        w1 = (prob + decay * a).astype(BF16)
        w2 = (prob * (b - delta) * scale + decay * b).astype(BF16)
        o_ref[0:W, at] = dot(w1[0:W], vx, 1, 0)
        o_ref[W:, at] = dot(w1[W:], v, 1, 0)
        qg_ref[0:W, at] = dot(w2[0:W], kx, 1, 0)
        qg_ref[W:, at] = dot(w2[W:], k, 1, 0)
        k_top = dot(w2[0:W], q[0:W], 0, 0)
        k_low = dot(w2[W:], q[W:], 0, 0)
        v_top = dot(w1[0:W], g[0:W], 0, 0)
        v_low = dot(w1[W:], g[W:], 0, 0)
        kg_ref[0:W, at] = k_low[0:W] + k_top[W:]
        kg_ref[W:, at] = k_low[W:]
        vg_ref[0:W, at] = v_low[0:W] + v_top[W:]
        vg_ref[W:, at] = v_low[W:]
        back_ref[0:W, at] = k_top[0:W].astype(BF16)
        back_ref[W : 2 * W, at] = v_top[0:W].astype(BF16)


def final_kernel(lin_scale, n_alias, sel_ref, q_ref, k_ref, v_ref, g_ref, ret_ref, gate_ref, st_ref, po_ref, pq_ref, pk_ref, pv_ref, *rest):
    o_ref, qg_ref, kg_ref, vg_ref = rest[n_alias:]
    rows, cols = cumulative(gate_ref[...])
    for j in range(HALF):
        at = slice(j * DH, (j + 1) * DH)
        last = rows[j : j + 1, DH - 1 : DH]
        head = jnp.exp(cols[:, j : j + 1]) * lin_scale
        tail = jnp.exp(last - cols[:, j : j + 1]) * lin_scale
        s = jnp.concatenate([st_ref[2 * j, 0:64, :], st_ref[2 * j + 1, 0:64, :]], axis=0)
        m = jnp.concatenate([st_ref[2 * j, 64:128, :], st_ref[2 * j + 1, 64:128, :]], axis=0)
        o_ref[:, at] = (po_ref[:, at] + head * dot(q_ref[:, at], s, 1, 0)).astype(BF16)
        qg_ref[:, at] = (pq_ref[:, at] + head * dot(g_ref[:, at], s, 1, 1)).astype(BF16)
        kg = pk_ref[:, at] + tail * dot(v_ref[:, at], m, 1, 1)
        vg = pv_ref[:, at] + tail * dot(k_ref[:, at], m, 1, 0)
        kg_ref[0:W, at] = kg[0:W].astype(BF16)
        kg_ref[W:, at] = (kg[W:] + ret_ref[0:W, at].astype(F32)).astype(BF16)
        vg_ref[0:W, at] = vg[0:W].astype(BF16)
        vg_ref[W:, at] = (vg[W:] + ret_ref[W : 2 * W, at].astype(F32)).astype(BF16)


def cost(flops, nbytes):
    return pl.CostEstimate(flops=int(flops), bytes_accessed=int(nbytes), transcendentals=0)


def half_specs(n):
    return [pl.BlockSpec((128, COLS), lambda i, sel: (0, sel[0])) for _ in range(n)]


GATE = pl.BlockSpec((HALF, DH), lambda i, sel: (sel[0], 0))


def whole(shape):
    return pl.BlockSpec(shape, lambda *_: (0,) * len(shape))


def local_states(sel, q, k, v, g, gates):
    return pl.pallas_call(
        states_kernel,
        out_shape=jax.ShapeDtypeStruct((PLANE, MSG, DH), BF16),
        grid_spec=pltpu.PrefetchScalarGridSpec(
            num_scalar_prefetch=1, grid=(1,), in_specs=half_specs(4) + [GATE], out_specs=whole((PLANE, MSG, DH))
        ),
        cost_estimate=cost(7e7, 1.6e6),
        name="local_states",
    )(sel, q, k, v, g, gates)


def small_call(body, name, scalar, arrays, outs):
    return pl.pallas_call(
        body,
        out_shape=tuple(jax.ShapeDtypeStruct(s, BF16) for s in outs),
        grid_spec=pltpu.PrefetchScalarGridSpec(
            num_scalar_prefetch=1,
            grid=(1,),
            in_specs=[whole(a.shape) for a in arrays],
            out_specs=tuple(whole(s) for s in outs),
        ),
        cost_estimate=cost(1e6, 2e6),
        name=name,
    )(scalar, *arrays)


def window(lin_scale, live, q, k, v, g, halo, gates):
    col = pl.BlockSpec((128, COLS), lambda i, s: (0, i))
    return pl.pallas_call(
        lambda *refs: window_kernel(lin_scale, *refs),
        out_shape=tuple(jax.ShapeDtypeStruct((128, 2048), F32) for _ in range(4)) + (jax.ShapeDtypeStruct((128, 2048), BF16),),
        grid_spec=pltpu.PrefetchScalarGridSpec(
            num_scalar_prefetch=1,
            grid=(2,),
            in_specs=[col] * 5 + [pl.BlockSpec((HALF, DH), lambda i, s: (i, 0))],
            out_specs=(col,) * 5,
        ),
        cost_estimate=cost(6e8, 8e6),
        name="window",
    )(live, q, k, v, g, halo, gates)


def finish(lin_scale, sel, q, k, v, g, ret, gates, states, parts, previous):
    n = len(previous)
    return pl.pallas_call(
        lambda *refs: final_kernel(lin_scale, n, *refs),
        out_shape=tuple(jax.ShapeDtypeStruct((128, 2048), BF16) for _ in range(4)),
        grid_spec=pltpu.PrefetchScalarGridSpec(
            num_scalar_prefetch=1,
            grid=(1,),
            in_specs=half_specs(5)
            + [GATE, whole(states.shape)]
            + half_specs(4)
            + [pl.BlockSpec(memory_space=pl.ANY)] * n,
            out_specs=tuple(half_specs(4)),
        ),
        input_output_aliases={12 + i: i for i in range(n)},
        cost_estimate=cost(3e8, 5e6),
        name="finish",
    )(sel, q, k, v, g, ret, gates, states, *parts, *previous)


def per_device(q, k, v, g, gates):
    lin_scale = (DH * q.shape[0] * 256) ** (-0.5)
    core = lax.axis_index("c")
    mine = core[None].astype(jnp.int32)
    theirs = 1 - mine
    z = lax.axis_index("z")[None].astype(jnp.int32)
    live = (lax.axis_index(AXES) > 0)[None].astype(jnp.int32)
    swap = [(0, 1), (1, 0)]

    sent = local_states(theirs, q, k, v, g, gates)
    other = lax.ppermute(sent, "c", swap)
    own = local_states(mine, q, k, v, g, gates)
    (chip,) = small_call(combine_kernel, "combine", mine, (own, other), [(PLANE, MSG, DH)])
    plane = lax.all_to_all(chip, ("x", "y"), 0, 0, tiled=True)

    halo = lax.ppermute(jnp.concatenate([k[-W:], v[-W:]], axis=0), AXES, [(i, i + 1) for i in range(255)])
    *parts, back = window(lin_scale, live, q, k, v, g, halo, gates)
    ret = lax.ppermute(back, AXES, [(i + 1, i) for i in range(255)])

    (total,) = small_call(lambda s, m, o: plane_kernel(m, o), "plane", z, (plane,), [(GRID[0], MSG, DH)])
    planes = lax.all_to_all(total, "z", 0, 0, tiled=True)
    (incoming,) = small_call(incoming_kernel, "incoming", z, (plane, planes), [(PLANE, DH, DH)])
    chip_in = lax.all_to_all(incoming, ("x", "y"), 0, 0, tiled=True)
    st_mine, st_theirs = small_call(hand_kernel, "hand", mine, (chip_in, own, other), [(PLANE, DH, DH)] * 2)
    st_other = lax.ppermute(st_theirs, "c", swap)
    outs = finish(lin_scale, mine, q, k, v, g, ret, gates, st_mine, parts, ())
    outs = finish(lin_scale, theirs, q, k, v, g, ret, gates, st_other, parts, outs)
    return outs


def solution(mesh):
    fine = Mesh(mesh.devices.reshape(GRID), AXES)
    rows = P(AXES, None)
    return jax.shard_map(
        per_device,
        mesh=fine,
        in_specs=(rows,) * 4 + (P(None, AXES),),
        out_specs=(rows,) * 4,
        check_vma=False,
    )
```

```python
import math

import jax
import jax.numpy as jnp
from jax import lax
from jax.experimental import pallas as pl
from jax.experimental.pallas import tpu as pltpu
from jax.sharding import Mesh
from jax.sharding import PartitionSpec as P


AXES = ("z", "x", "y", "c")
GRID = (8, 4, 4, 2)
PLANE = 16
W = 64
DH = 128
HALF = 8
COLS = HALF * DH
STEP = 2
WSTEP = 4
MSG = 144
F32 = jnp.float32
BF16 = jnp.bfloat16


def dot(a, b, ca, cb):
    return lax.dot_general(a, b, (((ca,), (cb,)), ((), ())), preferred_element_type=F32)


def cumulative(gates):
    n = gates.shape[1]
    i = lax.broadcasted_iota(jnp.int32, (n, n), 0)
    j = lax.broadcasted_iota(jnp.int32, (n, n), 1)
    upper = (i <= j).astype(F32)
    rows = lax.dot_general(gates, upper, (((1,), (0,)), ((), ())), precision=lax.Precision.HIGHEST, preferred_element_type=F32)
    return rows, rows.T


def decay_tile(d):
    d = jnp.broadcast_to(d, (16, DH))
    hi = d.astype(BF16).astype(F32)
    mid = (d - hi).astype(BF16).astype(F32)
    low = d - hi - mid
    row = lax.broadcasted_iota(jnp.int32, (16, DH), 0)
    zero = jnp.zeros_like(d)
    return jnp.where(row == 0, hi, jnp.where(row == 1, mid, jnp.where(row == 2, low, zero))).astype(BF16)


def decay_of(tile):
    return jnp.sum(tile.astype(F32), axis=0, keepdims=True)


def states_kernel(with_halo, sel_ref, q_hbm, k_hbm, v_hbm, g_hbm, gate_hbm, *rest):
    if with_halo:
        msg_ref, halo_ref, q_ref, k_ref, v_ref, g_ref, gate_ref, sems, gate_sem, halo_sem = rest
    else:
        msg_ref, q_ref, k_ref, v_ref, g_ref, gate_ref, sems, gate_sem = rest
    sel = sel_ref[0]
    gate_copy = pltpu.make_async_copy(gate_hbm.at[pl.ds(pl.multiple_of(sel * HALF, HALF), HALF)], gate_ref, gate_sem)
    gate_copy.start()
    copies = []
    for i in range(HALF // STEP):
        source = pl.ds(pl.multiple_of(sel * COLS + i * STEP * DH, STEP * DH), STEP * DH)
        target = slice(i * STEP * DH, (i + 1) * STEP * DH)
        copies.append([
            pltpu.make_async_copy(big.at[:, source], small.at[:, target], sems.at[i, n])
            for n, (big, small) in enumerate(((k_hbm, k_ref), (v_hbm, v_ref), (q_hbm, q_ref), (g_hbm, g_ref)))
        ])
    for step in copies:
        for copy in step:
            copy.start()
    if with_halo:
        halo_copies = [
            pltpu.make_async_copy(big.at[W : 2 * W], halo_ref.at[n * W : (n + 1) * W], halo_sem.at[n])
            for n, big in enumerate((k_hbm, v_hbm))
        ]
        for copy in halo_copies:
            copy.start()
    gate_copy.wait()
    rows, cols = cumulative(gate_ref[...])
    for j in range(HALF):
        if j % STEP == 0:
            for copy in copies[j // STEP]:
                copy.wait()
        at = slice(j * DH, (j + 1) * DH)
        last = rows[j : j + 1, DH - 1 : DH]
        head = jnp.exp(cols[:, j : j + 1])
        tail = jnp.exp(last - cols[:, j : j + 1])
        kt = (k_ref[:, at].astype(F32) * tail).astype(BF16)
        qh = (q_ref[:, at].astype(F32) * head).astype(BF16)
        s = dot(kt, v_ref[:, at], 0, 0).astype(BF16)
        g = dot(qh, g_ref[:, at], 0, 0).astype(BF16)
        d = decay_tile(jnp.exp(last))
        for r in range(2):
            part = slice(r * 64, (r + 1) * 64)
            msg_ref[2 * j + r, 0:64, :] = s[part]
            msg_ref[2 * j + r, 64:128, :] = g[part]
            msg_ref[2 * j + r, 128:144, :] = d
    if with_halo:
        for copy in halo_copies:
            copy.wait()


def combine_kernel(c_ref, own_ref, other_ref, out_ref, kept_ref):
    kept_ref[...] = other_ref[...]
    first = c_ref[0] == 0

    def body(a_ref, b_ref):
        for p in range(PLANE):
            da = decay_of(a_ref[p, 128:144, :])
            db = decay_of(b_ref[p, 128:144, :])
            out_ref[p, 0:64, :] = (db * a_ref[p, 0:64, :].astype(F32) + b_ref[p, 0:64, :].astype(F32)).astype(BF16)
            out_ref[p, 64:128, :] = (a_ref[p, 64:128, :].astype(F32) + da * b_ref[p, 64:128, :].astype(F32)).astype(BF16)
            out_ref[p, 128:144, :] = decay_tile(da * db)

    @pl.when(first)
    def _():
        body(own_ref, other_ref)

    @pl.when(jnp.logical_not(first))
    def _():
        body(other_ref, own_ref)


def plane_kernel(z_ref, msg_ref, out_ref):
    fwd = jnp.zeros((64, DH), F32)
    bwd = jnp.zeros((64, DH), F32)
    d = jnp.ones((1, DH), F32)
    for p in range(PLANE):
        b = PLANE - 1 - p
        dp = decay_of(msg_ref[p, 128:144, :])
        fwd = dp * fwd + msg_ref[p, 0:64, :].astype(F32)
        bwd = decay_of(msg_ref[b, 128:144, :]) * bwd + msg_ref[b, 64:128, :].astype(F32)
        d = d * dp
    tile = decay_tile(d)
    for i in range(GRID[0]):
        out_ref[i, 0:64, :] = jnp.where(i > z_ref[0], fwd, bwd).astype(BF16)
        out_ref[i, 64:80, :] = tile


def incoming_kernel(z_ref, msg_ref, planes_ref, out_ref):
    z = z_ref[0]
    n = GRID[0]
    fwd = jnp.zeros((64, DH), F32)
    bwd = jnp.zeros((64, DH), F32)
    for i in range(n):
        b = n - 1 - i
        new_f = decay_of(planes_ref[i, 64:80, :]) * fwd + planes_ref[i, 0:64, :].astype(F32)
        fwd = jnp.where(i < z, new_f, fwd)
        new_b = decay_of(planes_ref[b, 64:80, :]) * bwd + planes_ref[b, 0:64, :].astype(F32)
        bwd = jnp.where(b > z, new_b, bwd)
    for p in range(PLANE):
        b = PLANE - 1 - p
        out_ref[p, 0:64, :] = fwd.astype(BF16)
        out_ref[b, 64:128, :] = bwd.astype(BF16)
        fwd = decay_of(msg_ref[p, 128:144, :]) * fwd + msg_ref[p, 0:64, :].astype(F32)
        bwd = decay_of(msg_ref[b, 128:144, :]) * bwd + msg_ref[b, 64:128, :].astype(F32)


def hand_kernel(c_ref, chip_ref, own_ref, other_ref, mine_ref, theirs_ref):
    first = c_ref[0] == 0

    def body(is_first):
        for p in range(PLANE):
            fwd = chip_ref[p, 0:64, :]
            bwd = chip_ref[p, 64:128, :]
            inner = own_ref if is_first else other_ref
            outer = other_ref if is_first else own_ref
            late_f = (decay_of(inner[p, 128:144, :]) * fwd.astype(F32) + inner[p, 0:64, :].astype(F32)).astype(BF16)
            early_b = (decay_of(outer[p, 128:144, :]) * bwd.astype(F32) + outer[p, 64:128, :].astype(F32)).astype(BF16)
            early_ref = mine_ref if is_first else theirs_ref
            late_ref = theirs_ref if is_first else mine_ref
            early_ref[p, 0:64, :] = fwd
            early_ref[p, 64:128, :] = early_b
            late_ref[p, 0:64, :] = late_f
            late_ref[p, 64:128, :] = bwd

    @pl.when(first)
    def _():
        body(True)

    @pl.when(jnp.logical_not(first))
    def _():
        body(False)


def window_kernel(lin_scale, live_ref, q_hbm, k_hbm, v_hbm, g_hbm, halo_ref, gate_hbm, *rest):
    outs, row_ref = rest[:5], rest[5]
    q_ref, k_ref, v_ref, g_ref, *stages, gate_ref, sems, out_sems, gate_sem = rest[6:]
    o_ref, qg_ref, kg_ref, vg_ref, back_ref = stages
    gate_copy = pltpu.make_async_copy(gate_hbm, gate_ref, gate_sem)
    gate_copy.start()
    width = WSTEP * DH

    def copies(i):
        at = pl.ds(pl.multiple_of(i * width, width), width)
        return [
            pltpu.make_async_copy(big.at[:, at], small.at[:, at], sems.at[i, n])
            for n, (big, small) in enumerate(((q_hbm, q_ref), (k_hbm, k_ref), (v_hbm, v_ref), (g_hbm, g_ref)))
        ]

    def out_copies(i):
        at = pl.ds(pl.multiple_of(i * width, width), width)
        return [pltpu.make_async_copy(stage.at[:, at], out.at[:, at], out_sems.at[i, n]) for n, (stage, out) in enumerate(zip(stages, outs, strict=True))]

    for i in range(16 // WSTEP):
        for copy in copies(i):
            copy.start()
    live = live_ref[0] > 0
    t = lax.broadcasted_iota(jnp.int32, (DH, DH), 0)
    lane = lax.broadcasted_iota(jnp.int32, (DH, DH), 1)
    key = jnp.where(t < W, lane - W, lane)
    causal = (key >= 0) & (key <= t)
    banded = (key > t - W) & (key <= t) & ((key >= 0) | live)
    scale = DH**-0.5
    lin_bias = jnp.where(causal, math.log(lin_scale), -jnp.inf)
    win_bias = jnp.where(banded, 0.0, -jnp.inf)
    gate_copy.wait()
    row_ref[...] = cumulative(gate_ref[...])[0]

    def step(i, carry):
        for copy in copies(i):
            copy.wait()
        for j in range(WSTEP):
            at = pl.ds(pl.multiple_of(i * width + j * DH, DH), DH)
            q, k, v, g = q_ref[:, at], k_ref[:, at], v_ref[:, at], g_ref[:, at]
            kx = jnp.concatenate([halo_ref[0:W, at], k[0:W]], axis=0)
            vx = jnp.concatenate([halo_ref[W : 2 * W, at], v[0:W]], axis=0)
            a = jnp.concatenate([dot(q[0:W], kx, 1, 1), dot(q[W:], k, 1, 1)], axis=0)
            b = jnp.concatenate([dot(g[0:W], vx, 1, 1), dot(g[W:], v, 1, 1)], axis=0)
            row = jnp.broadcast_to(row_ref[pl.ds(i * WSTEP + j, 1), :], (DH, DH))
            shifted = jnp.concatenate([row[:W, W:], row[:W, :W]], axis=1)
            gap = row.T - jnp.concatenate([shifted, row[W:]], axis=0)
            decay = jnp.exp(gap + lin_bias)
            logits = a * scale + win_bias
            e = jnp.exp(logits - jnp.max(logits, axis=1, keepdims=True))
            inv = 1.0 / jnp.sum(e, axis=1, keepdims=True)
            delta = jnp.sum(e * b, axis=1, keepdims=True) * inv
            w1 = (e * inv + decay * a).astype(BF16)
            w2 = (e * (inv * scale) * (b - delta) + decay * b).astype(BF16)
            o_ref[0:W, at] = dot(w1[0:W], vx, 1, 0)
            o_ref[W:, at] = dot(w1[W:], v, 1, 0)
            qg_ref[0:W, at] = dot(w2[0:W], kx, 1, 0)
            qg_ref[W:, at] = dot(w2[W:], k, 1, 0)
            k_top = dot(w2[0:W], q[0:W], 0, 0)
            k_low = dot(w2[W:], q[W:], 0, 0)
            v_top = dot(w1[0:W], g[0:W], 0, 0)
            v_low = dot(w1[W:], g[W:], 0, 0)
            kg_ref[0:W, at] = k_low[0:W] + k_top[W:]
            kg_ref[W:, at] = k_low[W:]
            vg_ref[0:W, at] = v_low[0:W] + v_top[W:]
            vg_ref[W:, at] = v_low[W:]
            back_ref[0:W, at] = k_top[0:W].astype(BF16)
            back_ref[W : 2 * W, at] = v_top[0:W].astype(BF16)
        for copy in out_copies(i):
            copy.start()
        return carry

    lax.fori_loop(0, 16 // WSTEP, step, 0)
    for i in range(16 // WSTEP):
        for copy in out_copies(i):
            copy.wait()


def final_kernel(lin_scale, n_alias, sel_ref, q_ref, k_ref, v_ref, g_ref, ret_hbm, row_ref, st_ref, po_ref, pq_ref, pk_ref, pv_ref, *rest):
    outs = rest[n_alias : n_alias + 4]
    stage_ref, ret_ref, sems, ret_sem = rest[n_alias + 4 :]
    sel = sel_ref[0]
    ret_copy = pltpu.make_async_copy(ret_hbm.at[:, pl.ds(pl.multiple_of(sel * COLS, COLS), COLS)], ret_ref, ret_sem)
    ret_copy.start()
    rows = row_ref[pl.ds(pl.multiple_of(sel * HALF, HALF), HALF), :]
    heads = jnp.exp(rows).T * lin_scale
    tails = jnp.exp(rows[:, DH - 1 :] - rows).T * lin_scale
    width = STEP * DH
    copies = []

    def send(n, j):
        if j % STEP == STEP - 1:
            i = j // STEP
            target = pl.ds(pl.multiple_of(sel * COLS + i * width, width), width)
            copy = pltpu.make_async_copy(stage_ref.at[n, :, i * width : (i + 1) * width], outs[n].at[:, target], sems.at[i, n])
            copy.start()
            copies.append(copy)

    for j in range(HALF):
        at = pl.ds(pl.multiple_of(sel * COLS + j * DH, DH), DH)
        to = slice(j * DH, (j + 1) * DH)
        head = heads[:, j : j + 1]
        s = jnp.concatenate([st_ref[2 * j, 0:64, :], st_ref[2 * j + 1, 0:64, :]], axis=0)
        stage_ref[0, :, to] = (po_ref[:, at] + head * dot(q_ref[:, at], s, 1, 0)).astype(BF16)
        stage_ref[1, :, to] = (pq_ref[:, at] + head * dot(g_ref[:, at], s, 1, 1)).astype(BF16)
        send(0, j)
        send(1, j)
    ret_copy.wait()
    for j in range(HALF):
        at = pl.ds(pl.multiple_of(sel * COLS + j * DH, DH), DH)
        to = slice(j * DH, (j + 1) * DH)
        tail = tails[:, j : j + 1]
        m = jnp.concatenate([st_ref[2 * j, 64:128, :], st_ref[2 * j + 1, 64:128, :]], axis=0)
        kg = pk_ref[:, at] + tail * dot(v_ref[:, at], m, 1, 1)
        vg = pv_ref[:, at] + tail * dot(k_ref[:, at], m, 1, 0)
        stage_ref[2, 0:W, to] = kg[0:W].astype(BF16)
        stage_ref[2, W:, to] = (kg[W:] + ret_ref[0:W, to].astype(F32)).astype(BF16)
        stage_ref[3, 0:W, to] = vg[0:W].astype(BF16)
        stage_ref[3, W:, to] = (vg[W:] + ret_ref[W : 2 * W, to].astype(F32)).astype(BF16)
        send(2, j)
        send(3, j)
    for copy in copies:
        copy.wait()


def vmem(mib):
    return pltpu.CompilerParams(vmem_limit_bytes=mib << 20)


def cost(flops, nbytes):
    return pl.CostEstimate(flops=int(flops), bytes_accessed=int(nbytes), transcendentals=0)


IN_VMEM = pl.BlockSpec(memory_space=pltpu.VMEM)
IN_HBM = pl.BlockSpec(memory_space=pltpu.HBM)
IN_SMEM = pl.BlockSpec(memory_space=pltpu.SMEM)
DMA = pltpu.SemaphoreType.DMA


def local_states(sel, q, k, v, g, gates, with_halo):
    outs = [pltpu.VMEM((PLANE, MSG, DH), BF16)]
    sems = [DMA((HALF // STEP, 4)), DMA]
    if with_halo:
        outs.append(pltpu.VMEM((2 * W, 2048), BF16))
        sems.append(DMA((2,)))
    return pl.pallas_call(
        lambda *refs: states_kernel(with_halo, *refs),
        out_shape=tuple(outs),
        in_specs=[IN_SMEM] + [IN_HBM] * 5,
        out_specs=(IN_VMEM,) * len(outs),
        scratch_shapes=[pltpu.VMEM((128, COLS), BF16)] * 4 + [pltpu.VMEM((HALF, DH), F32)] + sems,
        cost_estimate=cost(7e7, 1.6e6),
        compiler_params=vmem(8),
        name="local_states",
    )(sel, q, k, v, g, gates)


def small_call(body, scalar, arrays, outs):
    return pl.pallas_call(
        body,
        out_shape=tuple(pltpu.VMEM(s, BF16) for s in outs),
        in_specs=[IN_SMEM] + [IN_VMEM] * len(arrays),
        out_specs=(IN_VMEM,) * len(outs),
        cost_estimate=cost(1e6, 2e6),
        compiler_params=vmem(4),
    )(scalar, *arrays)


def window(lin_scale, live, q, k, v, g, halo, gates):
    full = (128, 2048)
    steps = 16 // WSTEP
    return pl.pallas_call(
        lambda *refs: window_kernel(lin_scale, *refs),
        out_shape=tuple(pltpu.HBM(full, F32) for _ in range(4)) + (pltpu.HBM(full, BF16), pltpu.VMEM((16, DH), F32)),
        in_specs=[IN_SMEM] + [IN_HBM] * 4 + [IN_VMEM, IN_HBM],
        out_specs=(IN_HBM,) * 5 + (IN_VMEM,),
        scratch_shapes=[pltpu.VMEM(full, BF16)] * 4
        + [pltpu.VMEM(full, F32)] * 4
        + [pltpu.VMEM(full, BF16), pltpu.VMEM((16, DH), F32), DMA((steps, 4)), DMA((steps, 5)), DMA],
        cost_estimate=cost(6e8, 8e6),
        compiler_params=vmem(14),
        name="window",
    )(live, q, k, v, g, halo, gates)


def finish(lin_scale, sel, q, k, v, g, ret, rows, states, parts, previous):
    n = len(previous)
    return pl.pallas_call(
        lambda *refs: final_kernel(lin_scale, n, *refs),
        out_shape=tuple(pltpu.HBM((128, 2048), BF16) for _ in range(4)),
        in_specs=[IN_SMEM] + [IN_VMEM] * 4 + [IN_HBM] + [IN_VMEM] * 6 + [IN_HBM] * n,
        out_specs=(IN_HBM,) * 4,
        scratch_shapes=[pltpu.VMEM((4, 128, COLS), BF16), pltpu.VMEM((128, COLS), BF16), DMA((HALF // STEP, 4)), DMA],
        input_output_aliases={12 + i: i for i in range(n)},
        cost_estimate=cost(3e8, 5e6),
        compiler_params=vmem(8),
        name="finish",
    )(sel, q, k, v, g, ret, rows, states, *parts, *previous)


def per_device(q, k, v, g, gates):
    lin_scale = (DH * q.shape[0] * 256) ** (-0.5)
    core = lax.axis_index("c")
    mine = core[None].astype(jnp.int32)
    theirs = 1 - mine
    z = lax.axis_index("z")[None].astype(jnp.int32)
    live = (lax.axis_index(AXES) > 0)[None].astype(jnp.int32)
    swap = [(0, 1), (1, 0)]
    late = (q, k, v, g)
    q, k, v, g, gates = (pltpu.with_memory_space_constraint(a, pltpu.HBM) for a in (q, k, v, g, gates))

    sent, edge = local_states(theirs, q, k, v, g, gates, True)
    other = lax.ppermute(sent, "c", swap)
    halo = lax.ppermute(edge, AXES, [(i, i + 1) for i in range(255)])
    (own,) = local_states(mine, q, k, v, g, gates, False)
    chip, other = small_call(combine_kernel, mine, (own, other), [(PLANE, MSG, DH)] * 2)
    plane = lax.all_to_all(chip, ("x", "y"), 0, 0, tiled=True)
    *parts, back, sums = window(lin_scale, live, q, k, v, g, halo, gates)
    (total,) = small_call(plane_kernel, z, (plane,), [(GRID[0], 80, DH)])
    planes = lax.all_to_all(total, "z", 0, 0, tiled=True)
    ret = lax.ppermute(back, AXES, [(i + 1, i) for i in range(255)])
    (incoming,) = small_call(incoming_kernel, z, (plane, planes), [(PLANE, DH, DH)])
    chip_in = lax.all_to_all(incoming, ("x", "y"), 0, 0, tiled=True)
    st_mine, st_theirs = small_call(hand_kernel, mine, (chip_in, own, other), [(PLANE, DH, DH)] * 2)
    st_other = lax.ppermute(st_theirs, "c", swap)
    outs = finish(lin_scale, mine, *late, ret, sums, st_mine, parts, ())
    return finish(lin_scale, theirs, *late, ret, sums, st_other, parts, outs)


def solution(mesh):
    fine = Mesh(mesh.devices.reshape(GRID), AXES)
    rows = P(AXES, None)

    return jax.shard_map(
        per_device,
        mesh=fine,
        in_specs=(rows,) * 4 + (P(None, AXES),),
        out_specs=(rows,) * 4,
        check_vma=False,
    )
```

```python
import math

import jax
import jax.numpy as jnp
from jax import lax
from jax.experimental import pallas as pl
from jax.experimental.pallas import tpu as pltpu
from jax.sharding import Mesh
from jax.sharding import PartitionSpec as P


AXES = ("z", "x", "y", "c")
GRID = (8, 4, 4, 2)
PLANE = 16
W = 64
DH = 128
HALF = 8
COLS = HALF * DH
STEP = 8
OSTEP = 2
WSTEP = 16
GROUP = 8
MSG = 144
F32 = jnp.float32
BF16 = jnp.bfloat16


def dot(a, b, ca, cb):
    return lax.dot_general(a, b, (((ca,), (cb,)), ((), ())), preferred_element_type=F32)


def cumulative(gates):
    n = gates.shape[1]
    i = lax.broadcasted_iota(jnp.int32, (n, n), 0)
    j = lax.broadcasted_iota(jnp.int32, (n, n), 1)
    upper = (i <= j).astype(F32)
    return lax.dot_general(gates, upper, (((1,), (0,)), ((), ())), precision=lax.Precision.HIGHEST, preferred_element_type=F32)


def decay_tile(d):
    d = jnp.broadcast_to(d, (16, DH))
    hi = d.astype(BF16).astype(F32)
    mid = (d - hi).astype(BF16).astype(F32)
    low = d - hi - mid
    row = lax.broadcasted_iota(jnp.int32, (16, DH), 0)
    zero = jnp.zeros_like(d)
    return jnp.where(row == 0, hi, jnp.where(row == 1, mid, jnp.where(row == 2, low, zero))).astype(BF16)


def decay_of(tile):
    return jnp.sum(tile.astype(F32), axis=0, keepdims=True)


def states_kernel(with_halo, sel_ref, q_hbm, k_hbm, v_hbm, g_hbm, gate_hbm, *rest):
    if with_halo:
        msg_ref, halo_ref, q_ref, k_ref, v_ref, g_ref, gate_ref, sems, gate_sem, halo_sem = rest
    else:
        msg_ref, q_ref, k_ref, v_ref, g_ref, gate_ref, sems, gate_sem = rest
    sel = sel_ref[0]
    gate_copy = pltpu.make_async_copy(gate_hbm.at[pl.ds(pl.multiple_of(sel * HALF, HALF), HALF)], gate_ref, gate_sem)
    gate_copy.start()
    copies = []
    for i in range(HALF // STEP):
        source = pl.ds(pl.multiple_of(sel * COLS + i * STEP * DH, STEP * DH), STEP * DH)
        target = slice(i * STEP * DH, (i + 1) * STEP * DH)
        copies.append([
            pltpu.make_async_copy(big.at[:, source], small.at[:, target], sems.at[i, n])
            for n, (big, small) in enumerate(((k_hbm, k_ref), (v_hbm, v_ref), (q_hbm, q_ref), (g_hbm, g_ref)))
        ])
    for step in copies:
        for copy in step:
            copy.start()
    if with_halo:
        halo_copies = [
            pltpu.make_async_copy(big.at[W : 2 * W], halo_ref.at[n * W : (n + 1) * W], halo_sem.at[n])
            for n, big in enumerate((k_hbm, v_hbm))
        ]
        for copy in halo_copies:
            copy.start()
    gate_copy.wait()
    rows = cumulative(gate_ref[...])
    heads, tails = jnp.exp(rows), jnp.exp(rows[:, DH - 1 :] - rows)
    for j in range(HALF):
        if j % GROUP == 0:
            for step in copies[j // STEP : (j + GROUP) // STEP]:
                for copy in step:
                    copy.wait()
        at = slice(j * DH, (j + 1) * DH)
        last = rows[j : j + 1, DH - 1 : DH]
        kt = (k_ref[:, at].T.astype(F32) * tails[j : j + 1]).astype(BF16)
        qh = (q_ref[:, at].T.astype(F32) * heads[j : j + 1]).astype(BF16)
        s = dot(kt, v_ref[:, at], 1, 0).astype(BF16)
        g = dot(qh, g_ref[:, at], 1, 0).astype(BF16)
        d = decay_tile(jnp.exp(last))
        for r in range(2):
            part = slice(r * 64, (r + 1) * 64)
            msg_ref[2 * j + r, 0:64, :] = s[part]
            msg_ref[2 * j + r, 64:128, :] = g[part]
            msg_ref[2 * j + r, 128:144, :] = d
    if with_halo:
        for copy in halo_copies:
            copy.wait()


def combine_kernel(c_ref, own_ref, other_ref, out_ref, kept_ref):
    kept_ref[...] = other_ref[...]
    first = c_ref[0] == 0

    def body(a_ref, b_ref):
        for p in range(PLANE):
            da = decay_of(a_ref[p, 128:144, :])
            db = decay_of(b_ref[p, 128:144, :])
            out_ref[p, 0:64, :] = (db * a_ref[p, 0:64, :].astype(F32) + b_ref[p, 0:64, :].astype(F32)).astype(BF16)
            out_ref[p, 64:128, :] = (a_ref[p, 64:128, :].astype(F32) + da * b_ref[p, 64:128, :].astype(F32)).astype(BF16)
            out_ref[p, 128:144, :] = decay_tile(da * db)

    @pl.when(first)
    def _():
        body(own_ref, other_ref)

    @pl.when(jnp.logical_not(first))
    def _():
        body(other_ref, own_ref)


def plane_kernel(z_ref, msg_ref, out_ref):
    fwd = jnp.zeros((64, DH), F32)
    bwd = jnp.zeros((64, DH), F32)
    d = jnp.ones((1, DH), F32)
    for p in range(PLANE):
        b = PLANE - 1 - p
        dp = decay_of(msg_ref[p, 128:144, :])
        fwd = dp * fwd + msg_ref[p, 0:64, :].astype(F32)
        bwd = decay_of(msg_ref[b, 128:144, :]) * bwd + msg_ref[b, 64:128, :].astype(F32)
        d = d * dp
    tile = decay_tile(d)
    for i in range(GRID[0]):
        out_ref[i, 0:64, :] = jnp.where(i > z_ref[0], fwd, bwd).astype(BF16)
        out_ref[i, 64:80, :] = tile


def incoming_kernel(z_ref, msg_ref, planes_ref, out_ref):
    z = z_ref[0]
    n = GRID[0]
    fwd = jnp.zeros((64, DH), F32)
    bwd = jnp.zeros((64, DH), F32)
    for i in range(n):
        b = n - 1 - i
        new_f = decay_of(planes_ref[i, 64:80, :]) * fwd + planes_ref[i, 0:64, :].astype(F32)
        fwd = jnp.where(i < z, new_f, fwd)
        new_b = decay_of(planes_ref[b, 64:80, :]) * bwd + planes_ref[b, 0:64, :].astype(F32)
        bwd = jnp.where(b > z, new_b, bwd)
    for p in range(PLANE):
        b = PLANE - 1 - p
        out_ref[p, 0:64, :] = fwd.astype(BF16)
        out_ref[b, 64:128, :] = bwd.astype(BF16)
        fwd = decay_of(msg_ref[p, 128:144, :]) * fwd + msg_ref[p, 0:64, :].astype(F32)
        bwd = decay_of(msg_ref[b, 128:144, :]) * bwd + msg_ref[b, 64:128, :].astype(F32)


def hand_kernel(c_ref, chip_ref, own_ref, other_ref, mine_ref, theirs_ref):
    first = c_ref[0] == 0

    def body(is_first):
        for p in range(PLANE):
            fwd = chip_ref[p, 0:64, :]
            bwd = chip_ref[p, 64:128, :]
            inner = own_ref if is_first else other_ref
            outer = other_ref if is_first else own_ref
            late_f = (decay_of(inner[p, 128:144, :]) * fwd.astype(F32) + inner[p, 0:64, :].astype(F32)).astype(BF16)
            early_b = (decay_of(outer[p, 128:144, :]) * bwd.astype(F32) + outer[p, 64:128, :].astype(F32)).astype(BF16)
            early_ref = mine_ref if is_first else theirs_ref
            late_ref = theirs_ref if is_first else mine_ref
            early_ref[p, 0:64, :] = fwd
            early_ref[p, 64:128, :] = early_b
            late_ref[p, 0:64, :] = late_f
            late_ref[p, 64:128, :] = bwd

    @pl.when(first)
    def _():
        body(True)

    @pl.when(jnp.logical_not(first))
    def _():
        body(False)


def window_kernel(lin_scale, live_ref, q_hbm, k_hbm, v_hbm, g_hbm, halo_ref, gate_hbm, *rest):
    outs, row_ref = rest[:5], rest[5]
    q_ref, k_ref, v_ref, g_ref, *stages, a_ref, b_ref, w1_ref, w2_ref, lin_ref, win_ref, gate_ref, sems, out_sems, gate_sem = rest[6:]
    o_ref, qg_ref, kg_ref, vg_ref, back_ref = stages
    gate_copy = pltpu.make_async_copy(gate_hbm, gate_ref, gate_sem)
    gate_copy.start()
    width = WSTEP * DH

    def copies(i):
        at = pl.ds(pl.multiple_of(i * width, width), width)
        return [
            pltpu.make_async_copy(big.at[:, at], small.at[:, at], sems.at[i, n])
            for n, (big, small) in enumerate(((q_hbm, q_ref), (k_hbm, k_ref), (v_hbm, v_ref), (g_hbm, g_ref)))
        ]

    def out_copies(i):
        at = pl.ds(pl.multiple_of(i * 2 * DH, 2 * DH), 2 * DH)
        return [pltpu.make_async_copy(stage.at[:, at], out.at[:, at], out_sems.at[i, n]) for n, (stage, out) in enumerate(zip(stages, outs, strict=True))]

    for i in range(16 // WSTEP):
        for copy in copies(i):
            copy.start()
    live = live_ref[0] > 0
    t = lax.broadcasted_iota(jnp.int32, (DH, DH), 0)
    lane = lax.broadcasted_iota(jnp.int32, (DH, DH), 1)
    key = jnp.where(t < W, lane - W, lane)
    causal = (key >= 0) & (key <= t)
    banded = (key > t - W) & (key <= t) & ((key >= 0) | live)
    scale = DH**-0.5
    lin_ref[...] = jnp.where(causal, math.log(lin_scale), -jnp.inf)
    win_ref[...] = jnp.where(banded, 0.0, -jnp.inf)
    gate_copy.wait()
    row_ref[...] = cumulative(gate_ref[...])

    def step(i, carry):
        for copy in copies(i):
            copy.wait()
        heads = [pl.ds(pl.multiple_of(i * width + j * DH, DH), DH) for j in range(WSTEP)]
        for j, at in enumerate(heads):
            q, k, v, g = q_ref[:, at], k_ref[:, at], v_ref[:, at], g_ref[:, at]
            kx = jnp.concatenate([halo_ref[0:W, at], k[0:W]], axis=0)
            vx = jnp.concatenate([halo_ref[W : 2 * W, at], v[0:W]], axis=0)
            a_ref[j, 0:W] = dot(q[0:W], kx, 1, 1)
            a_ref[j, W:] = dot(q[W:], k, 1, 1)
            b_ref[j, 0:W] = dot(g[0:W], vx, 1, 1)
            b_ref[j, W:] = dot(g[W:], v, 1, 1)
        rows = row_ref[pl.ds(i * WSTEP, WSTEP), :]
        cols = rows.T
        for j in range(WSTEP):
            row = rows[j : j + 1, :]
            shifted = jnp.concatenate([row[:, W:], row[:, :W]], axis=1)
            keys = jnp.concatenate([jnp.broadcast_to(shifted, (W, DH)), jnp.broadcast_to(row, (W, DH))], axis=0)
            a, b = a_ref[j], b_ref[j]
            decay = jnp.exp(cols[:, j : j + 1] - keys + lin_ref[...])
            logits = a * scale + win_ref[...]
            e = jnp.exp(logits - jnp.max(logits, axis=1, keepdims=True))
            inv = 1.0 / jnp.sum(e, axis=1, keepdims=True)
            delta = jnp.sum(e * b, axis=1, keepdims=True) * inv
            w1_ref[j] = (e * inv + decay * a).astype(BF16)
            w2_ref[j] = (e * (inv * scale) * (b - delta) + decay * b).astype(BF16)
        for j, at in enumerate(heads):
            q, k, v, g = q_ref[:, at], k_ref[:, at], v_ref[:, at], g_ref[:, at]
            kx = jnp.concatenate([halo_ref[0:W, at], k[0:W]], axis=0)
            vx = jnp.concatenate([halo_ref[W : 2 * W, at], v[0:W]], axis=0)
            w1, w2 = w1_ref[j], w2_ref[j]
            o_ref[0:W, at] = dot(w1[0:W], vx, 1, 0)
            o_ref[W:, at] = dot(w1[W:], v, 1, 0)
            qg_ref[0:W, at] = dot(w2[0:W], kx, 1, 0)
            qg_ref[W:, at] = dot(w2[W:], k, 1, 0)
            k_top = dot(w2[0:W], q[0:W], 0, 0)
            k_low = dot(w2[W:], q[W:], 0, 0)
            v_top = dot(w1[0:W], g[0:W], 0, 0)
            v_low = dot(w1[W:], g[W:], 0, 0)
            kg_ref[0:W, at] = k_low[0:W] + k_top[W:]
            kg_ref[W:, at] = k_low[W:]
            vg_ref[0:W, at] = v_low[0:W] + v_top[W:]
            vg_ref[W:, at] = v_low[W:]
            back_ref[0:W, at] = k_top[0:W].astype(BF16)
            back_ref[W : 2 * W, at] = v_top[0:W].astype(BF16)
            if j % 2 == 1:
                for copy in out_copies(i * (WSTEP // 2) + j // 2):
                    copy.start()
        return carry

    lax.fori_loop(0, 16 // WSTEP, step, 0)
    for i in range(8):
        for copy in out_copies(i):
            copy.wait()


def final_kernel(lin_scale, n_alias, sel_ref, q_ref, k_hbm, v_hbm, g_ref, ret_hbm, row_ref, st_ref, po_ref, pq_ref, pk_hbm, pv_hbm, *rest):
    outs = rest[n_alias : n_alias + 4]
    stage_ref, k_ref, v_ref, ret_ref, pk_ref, pv_ref, sems, in_sems = rest[n_alias + 4 :]
    sel = sel_ref[0]
    half = pl.ds(pl.multiple_of(sel * COLS, COLS), COLS)
    late = [
        pltpu.make_async_copy(big.at[:, half], small, in_sems.at[n])
        for n, (big, small) in enumerate(((v_hbm, v_ref), (pk_hbm, pk_ref), (k_hbm, k_ref), (pv_hbm, pv_ref), (ret_hbm, ret_ref)))
    ]
    for copy in late:
        copy.start()
    rows = row_ref[pl.ds(pl.multiple_of(sel * HALF, HALF), HALF), :]
    heads = jnp.exp(rows).T * lin_scale
    tails = jnp.exp(rows[:, DH - 1 :] - rows).T * lin_scale
    width = OSTEP * DH
    copies = []

    def send(n, j):
        if j % OSTEP == OSTEP - 1:
            i = j // OSTEP
            target = pl.ds(pl.multiple_of(sel * COLS + i * width, width), width)
            copy = pltpu.make_async_copy(stage_ref.at[n, :, i * width : (i + 1) * width], outs[n].at[:, target], sems.at[i, n])
            copy.start()
            copies.append(copy)

    for j in range(HALF):
        at = pl.ds(pl.multiple_of(sel * COLS + j * DH, DH), DH)
        to = slice(j * DH, (j + 1) * DH)
        head = heads[:, j : j + 1]
        s = jnp.concatenate([st_ref[2 * j, 0:64, :], st_ref[2 * j + 1, 0:64, :]], axis=0)
        stage_ref[0, :, to] = (po_ref[:, at] + head * dot(q_ref[:, at], s, 1, 0)).astype(BF16)
        stage_ref[1, :, to] = (pq_ref[:, at] + head * dot(g_ref[:, at], s, 1, 1)).astype(BF16)
        send(0, j)
        send(1, j)
    for copy in late:
        copy.wait()
    for j in range(HALF):
        to = slice(j * DH, (j + 1) * DH)
        tail = tails[:, j : j + 1]
        m = jnp.concatenate([st_ref[2 * j, 64:128, :], st_ref[2 * j + 1, 64:128, :]], axis=0)
        kg = pk_ref[:, to] + tail * dot(v_ref[:, to], m, 1, 1)
        vg = pv_ref[:, to] + tail * dot(k_ref[:, to], m, 1, 0)
        stage_ref[2, 0:W, to] = kg[0:W].astype(BF16)
        stage_ref[2, W:, to] = (kg[W:] + ret_ref[0:W, to].astype(F32)).astype(BF16)
        stage_ref[3, 0:W, to] = vg[0:W].astype(BF16)
        stage_ref[3, W:, to] = (vg[W:] + ret_ref[W : 2 * W, to].astype(F32)).astype(BF16)
        send(2, j)
        send(3, j)
    for copy in copies:
        copy.wait()


def vmem(mib):
    return pltpu.CompilerParams(vmem_limit_bytes=mib << 20)


def cost(flops, nbytes):
    return pl.CostEstimate(flops=int(flops), bytes_accessed=int(nbytes), transcendentals=0)


IN_VMEM = pl.BlockSpec(memory_space=pltpu.VMEM)
IN_HBM = pl.BlockSpec(memory_space=pltpu.HBM)
IN_SMEM = pl.BlockSpec(memory_space=pltpu.SMEM)
DMA = pltpu.SemaphoreType.DMA


def local_states(sel, q, k, v, g, gates, with_halo):
    outs = [pltpu.VMEM((PLANE, MSG, DH), BF16)]
    sems = [DMA((HALF // STEP, 4)), DMA]
    if with_halo:
        outs.append(pltpu.VMEM((2 * W, 2048), BF16))
        sems.append(DMA((2,)))
    return pl.pallas_call(
        lambda *refs: states_kernel(with_halo, *refs),
        out_shape=tuple(outs),
        in_specs=[IN_SMEM] + [IN_HBM] * 5,
        out_specs=(IN_VMEM,) * len(outs),
        scratch_shapes=[pltpu.VMEM((128, COLS), BF16)] * 4 + [pltpu.VMEM((HALF, DH), F32)] + sems,
        cost_estimate=cost(7e7, 1.6e6),
        compiler_params=vmem(8),
        name="local_states",
    )(sel, q, k, v, g, gates)


def small_call(body, scalar, arrays, outs):
    return pl.pallas_call(
        body,
        out_shape=tuple(pltpu.VMEM(s, BF16) for s in outs),
        in_specs=[IN_SMEM] + [IN_VMEM] * len(arrays),
        out_specs=(IN_VMEM,) * len(outs),
        cost_estimate=cost(1e6, 2e6),
        compiler_params=vmem(4),
    )(scalar, *arrays)


def window(lin_scale, live, q, k, v, g, halo, gates):
    full = (128, 2048)
    steps = 16 // WSTEP
    return pl.pallas_call(
        lambda *refs: window_kernel(lin_scale, *refs),
        out_shape=tuple(pltpu.HBM(full, F32) for _ in range(4)) + (pltpu.HBM(full, BF16), pltpu.VMEM((16, DH), F32)),
        in_specs=[IN_SMEM] + [IN_HBM] * 4 + [IN_VMEM, IN_HBM],
        out_specs=(IN_HBM,) * 5 + (IN_VMEM,),
        scratch_shapes=[pltpu.VMEM(full, BF16)] * 4
        + [pltpu.VMEM(full, F32)] * 4
        + [pltpu.VMEM(full, BF16)]
        + [pltpu.VMEM((WSTEP, DH, DH), t) for t in (F32, F32, BF16, BF16)]
        + [pltpu.VMEM((DH, DH), F32)] * 2
        + [pltpu.VMEM((16, DH), F32), DMA((steps, 4)), DMA((8, 5)), DMA],
        cost_estimate=cost(6e8, 8e6),
        compiler_params=vmem(14),
        name="window",
    )(live, q, k, v, g, halo, gates)


def finish(lin_scale, sel, q, k, v, g, ret, rows, states, parts, previous):
    n = len(previous)
    return pl.pallas_call(
        lambda *refs: final_kernel(lin_scale, n, *refs),
        out_shape=tuple(pltpu.HBM((128, 2048), BF16) for _ in range(4)),
        in_specs=[IN_SMEM, IN_VMEM, IN_HBM, IN_HBM, IN_VMEM, IN_HBM] + [IN_VMEM] * 4 + [IN_HBM] * (2 + n),
        out_specs=(IN_HBM,) * 4,
        scratch_shapes=[pltpu.VMEM((4, 128, COLS), BF16)] + [pltpu.VMEM((128, COLS), BF16)] * 3 + [pltpu.VMEM((128, COLS), F32)] * 2 + [DMA((HALF // OSTEP, 4)), DMA((5,))],
        input_output_aliases={12 + i: i for i in range(n)},
        cost_estimate=cost(3e8, 5e6),
        compiler_params=vmem(8),
        name="finish",
    )(sel, q, k, v, g, ret, rows, states, *parts, *previous)


def per_device(q, k, v, g, gates):
    lin_scale = (DH * q.shape[0] * 256) ** (-0.5)
    core = lax.axis_index("c")
    mine = core[None].astype(jnp.int32)
    theirs = 1 - mine
    z = lax.axis_index("z")[None].astype(jnp.int32)
    live = (lax.axis_index(AXES) > 0)[None].astype(jnp.int32)
    swap = [(0, 1), (1, 0)]
    q_late, g_late = q, g
    q, k, v, g, gates = (pltpu.with_memory_space_constraint(a, pltpu.HBM) for a in (q, k, v, g, gates))

    sent, edge = local_states(theirs, q, k, v, g, gates, True)
    other = lax.ppermute(sent, "c", swap)
    halo = lax.ppermute(edge, AXES, [(i, i + 1) for i in range(255)])
    (own,) = local_states(mine, q, k, v, g, gates, False)
    chip, other = small_call(combine_kernel, mine, (own, other), [(PLANE, MSG, DH)] * 2)
    plane = lax.all_to_all(chip, ("x", "y"), 0, 0, tiled=True)
    *parts, back, sums = window(lin_scale, live, q, k, v, g, halo, gates)
    (total,) = small_call(plane_kernel, z, (plane,), [(GRID[0], 80, DH)])
    planes = lax.all_to_all(total, "z", 0, 0, tiled=True)
    ret = lax.ppermute(back, AXES, [(i + 1, i) for i in range(255)])
    (incoming,) = small_call(incoming_kernel, z, (plane, planes), [(PLANE, DH, DH)])
    chip_in = lax.all_to_all(incoming, ("x", "y"), 0, 0, tiled=True)
    st_mine, st_theirs = small_call(hand_kernel, mine, (chip_in, own, other), [(PLANE, DH, DH)] * 2)
    st_other = lax.ppermute(st_theirs, "c", swap)
    parts[2:] = [pltpu.with_memory_space_constraint(a, pltpu.HBM) for a in parts[2:]]
    outs = finish(lin_scale, mine, q_late, k, v, g_late, ret, sums, st_mine, parts, ())
    return finish(lin_scale, theirs, q_late, k, v, g_late, ret, sums, st_other, parts, outs)


def solution(mesh):
    fine = Mesh(mesh.devices.reshape(GRID), AXES)
    rows = P(AXES, None)

    return jax.shard_map(
        per_device,
        mesh=fine,
        in_specs=(rows,) * 4 + (P(None, AXES),),
        out_specs=(rows,) * 4,
        check_vma=False,
    )
```

```python
import math

import jax
import jax.numpy as jnp
from jax import lax
from jax.experimental import pallas as pl
from jax.experimental.pallas import tpu as pltpu
from jax.sharding import Mesh
from jax.sharding import PartitionSpec as P


AXES = ("z", "x", "y", "c")
GRID = (8, 4, 4, 2)
PLANE = 16
W = 64
DH = 128
HALF = 8
COLS = HALF * DH
STEP = 8
OSTEP = 2
WSTEP = 16
GROUP = 8
MSG = 144
F32 = jnp.float32
BF16 = jnp.bfloat16


def dot(a, b, ca, cb):
    return lax.dot_general(a, b, (((ca,), (cb,)), ((), ())), preferred_element_type=F32)


def cumulative(gates):
    n = gates.shape[1]
    i = lax.broadcasted_iota(jnp.int32, (n, n), 0)
    j = lax.broadcasted_iota(jnp.int32, (n, n), 1)
    upper = (i <= j).astype(F32)
    return lax.dot_general(gates, upper, (((1,), (0,)), ((), ())), precision=lax.Precision.HIGHEST, preferred_element_type=F32)


def decay_tile(d):
    d = jnp.broadcast_to(d, (16, DH))
    hi = d.astype(BF16).astype(F32)
    mid = (d - hi).astype(BF16).astype(F32)
    low = d - hi - mid
    row = lax.broadcasted_iota(jnp.int32, (16, DH), 0)
    zero = jnp.zeros_like(d)
    return jnp.where(row == 0, hi, jnp.where(row == 1, mid, jnp.where(row == 2, low, zero))).astype(BF16)


def decay_of(tile):
    return jnp.sum(tile.astype(F32), axis=0, keepdims=True)


def states_kernel(with_halo, sel_ref, q_hbm, k_hbm, v_hbm, g_hbm, gate_hbm, *rest):
    if with_halo:
        msg_ref, halo_ref, q_ref, k_ref, v_ref, g_ref, gate_ref, sems, gate_sem, halo_sem = rest
    else:
        msg_ref, q_ref, k_ref, v_ref, g_ref, gate_ref, sems, gate_sem = rest
    sel = sel_ref[0]
    gate_copy = pltpu.make_async_copy(gate_hbm.at[pl.ds(pl.multiple_of(sel * HALF, HALF), HALF)], gate_ref, gate_sem)
    gate_copy.start()
    copies = []
    for i in range(HALF // STEP):
        source = pl.ds(pl.multiple_of(sel * COLS + i * STEP * DH, STEP * DH), STEP * DH)
        target = slice(i * STEP * DH, (i + 1) * STEP * DH)
        copies.append([
            pltpu.make_async_copy(big.at[:, source], small.at[:, target], sems.at[i, n])
            for n, (big, small) in enumerate(((k_hbm, k_ref), (v_hbm, v_ref), (q_hbm, q_ref), (g_hbm, g_ref)))
        ])
    for step in copies:
        for copy in step:
            copy.start()
    if with_halo:
        halo_copies = [
            pltpu.make_async_copy(big.at[W : 2 * W], halo_ref.at[n * W : (n + 1) * W], halo_sem.at[n])
            for n, big in enumerate((k_hbm, v_hbm))
        ]
        for copy in halo_copies:
            copy.start()
    gate_copy.wait()
    rows = cumulative(gate_ref[...])
    heads, tails = jnp.exp(rows), jnp.exp(rows[:, DH - 1 :] - rows)
    for j in range(HALF):
        if j % GROUP == 0:
            for step in copies[j // STEP : (j + GROUP) // STEP]:
                for copy in step:
                    copy.wait()
        at = slice(j * DH, (j + 1) * DH)
        last = rows[j : j + 1, DH - 1 : DH]
        kt = (k_ref[:, at].T.astype(F32) * tails[j : j + 1]).astype(BF16)
        qh = (q_ref[:, at].T.astype(F32) * heads[j : j + 1]).astype(BF16)
        s = dot(kt, v_ref[:, at], 1, 0).astype(BF16)
        g = dot(qh, g_ref[:, at], 1, 0).astype(BF16)
        d = decay_tile(jnp.exp(last))
        for r in range(2):
            part = slice(r * 64, (r + 1) * 64)
            msg_ref[2 * j + r, 0:64, :] = s[part]
            msg_ref[2 * j + r, 64:128, :] = g[part]
            msg_ref[2 * j + r, 128:144, :] = d
    if with_halo:
        for copy in halo_copies:
            copy.wait()


def combine_kernel(c_ref, own_ref, other_ref, out_ref, kept_ref):
    kept_ref[...] = other_ref[...]
    first = c_ref[0] == 0

    def body(a_ref, b_ref):
        for p in range(PLANE):
            da = decay_of(a_ref[p, 128:144, :])
            db = decay_of(b_ref[p, 128:144, :])
            out_ref[p, 0:64, :] = (db * a_ref[p, 0:64, :].astype(F32) + b_ref[p, 0:64, :].astype(F32)).astype(BF16)
            out_ref[p, 64:128, :] = (a_ref[p, 64:128, :].astype(F32) + da * b_ref[p, 64:128, :].astype(F32)).astype(BF16)
            out_ref[p, 128:144, :] = decay_tile(da * db)

    @pl.when(first)
    def _():
        body(own_ref, other_ref)

    @pl.when(jnp.logical_not(first))
    def _():
        body(other_ref, own_ref)


def plane_kernel(z_ref, msg_ref, out_ref):
    fwd = jnp.zeros((64, DH), F32)
    bwd = jnp.zeros((64, DH), F32)
    d = jnp.ones((1, DH), F32)
    for p in range(PLANE):
        b = PLANE - 1 - p
        dp = decay_of(msg_ref[p, 128:144, :])
        fwd = dp * fwd + msg_ref[p, 0:64, :].astype(F32)
        bwd = decay_of(msg_ref[b, 128:144, :]) * bwd + msg_ref[b, 64:128, :].astype(F32)
        d = d * dp
    tile = decay_tile(d)
    for i in range(GRID[0]):
        out_ref[i, 0:64, :] = jnp.where(i > z_ref[0], fwd, bwd).astype(BF16)
        out_ref[i, 64:80, :] = tile


def incoming_kernel(z_ref, msg_ref, planes_ref, out_ref):
    z = z_ref[0]
    n = GRID[0]
    fwd = jnp.zeros((64, DH), F32)
    bwd = jnp.zeros((64, DH), F32)
    for i in range(n):
        b = n - 1 - i
        new_f = decay_of(planes_ref[i, 64:80, :]) * fwd + planes_ref[i, 0:64, :].astype(F32)
        fwd = jnp.where(i < z, new_f, fwd)
        new_b = decay_of(planes_ref[b, 64:80, :]) * bwd + planes_ref[b, 0:64, :].astype(F32)
        bwd = jnp.where(b > z, new_b, bwd)
    for p in range(PLANE):
        b = PLANE - 1 - p
        out_ref[p, 0:64, :] = fwd.astype(BF16)
        out_ref[b, 64:128, :] = bwd.astype(BF16)
        fwd = decay_of(msg_ref[p, 128:144, :]) * fwd + msg_ref[p, 0:64, :].astype(F32)
        bwd = decay_of(msg_ref[b, 128:144, :]) * bwd + msg_ref[b, 64:128, :].astype(F32)


def hand_kernel(c_ref, chip_ref, own_ref, other_ref, mine_ref, theirs_ref):
    first = c_ref[0] == 0

    def body(is_first):
        for p in range(PLANE):
            fwd = chip_ref[p, 0:64, :]
            bwd = chip_ref[p, 64:128, :]
            inner = own_ref if is_first else other_ref
            outer = other_ref if is_first else own_ref
            late_f = (decay_of(inner[p, 128:144, :]) * fwd.astype(F32) + inner[p, 0:64, :].astype(F32)).astype(BF16)
            early_b = (decay_of(outer[p, 128:144, :]) * bwd.astype(F32) + outer[p, 64:128, :].astype(F32)).astype(BF16)
            early_ref = mine_ref if is_first else theirs_ref
            late_ref = theirs_ref if is_first else mine_ref
            early_ref[p, 0:64, :] = fwd
            early_ref[p, 64:128, :] = early_b
            late_ref[p, 0:64, :] = late_f
            late_ref[p, 64:128, :] = bwd

    @pl.when(first)
    def _():
        body(True)

    @pl.when(jnp.logical_not(first))
    def _():
        body(False)


def window_kernel(lin_scale, live_ref, q_hbm, k_hbm, v_hbm, g_hbm, halo_ref, gate_hbm, *rest):
    parts_hbm, inputs_hbm, back_hbm, row_ref = rest[:4]
    inputs_ref, parts_ref, back_ref, a_ref, b_ref, w1_ref, w2_ref, lin_ref, win_ref, gate_ref, sems, out_sems, gate_sem, kept_sem = rest[4:]
    q_ref, k_ref, v_ref, g_ref = (inputs_ref.at[n] for n in range(4))
    o_ref, qg_ref, kg_ref, vg_ref = (parts_ref.at[n] for n in range(4))
    kept = pltpu.make_async_copy(inputs_ref, inputs_hbm, kept_sem)
    gate_copy = pltpu.make_async_copy(gate_hbm, gate_ref, gate_sem)
    gate_copy.start()
    width = WSTEP * DH

    def copies(i):
        at = pl.ds(pl.multiple_of(i * width, width), width)
        return [
            pltpu.make_async_copy(big.at[:, at], small.at[:, at], sems.at[i, n])
            for n, (big, small) in enumerate(((q_hbm, q_ref), (k_hbm, k_ref), (v_hbm, v_ref), (g_hbm, g_ref)))
        ]

    def out_copies(i):
        at = pl.ds(pl.multiple_of(i * 2 * DH, 2 * DH), 2 * DH)
        return [
            pltpu.make_async_copy(parts_ref.at[:, :, at], parts_hbm.at[:, :, at], out_sems.at[i, 0]),
            pltpu.make_async_copy(back_ref.at[:, at], back_hbm.at[:, at], out_sems.at[i, 1]),
        ]

    for i in range(16 // WSTEP):
        for copy in copies(i):
            copy.start()
    live = live_ref[0] > 0
    t = lax.broadcasted_iota(jnp.int32, (DH, DH), 0)
    lane = lax.broadcasted_iota(jnp.int32, (DH, DH), 1)
    key = jnp.where(t < W, lane - W, lane)
    causal = (key >= 0) & (key <= t)
    banded = (key > t - W) & (key <= t) & ((key >= 0) | live)
    scale = DH**-0.5
    lin_ref[...] = jnp.where(causal, math.log(lin_scale), -jnp.inf)
    win_ref[...] = jnp.where(banded, 0.0, -jnp.inf)
    gate_copy.wait()
    row_ref[...] = cumulative(gate_ref[...])

    def step(i, carry):
        for copy in copies(i):
            copy.wait()
        if WSTEP == 16:
            kept.start()
        heads = [pl.ds(pl.multiple_of(i * width + j * DH, DH), DH) for j in range(WSTEP)]
        for j, at in enumerate(heads):
            q, k, v, g = q_ref[:, at], k_ref[:, at], v_ref[:, at], g_ref[:, at]
            kx = jnp.concatenate([halo_ref[0:W, at], k[0:W]], axis=0)
            vx = jnp.concatenate([halo_ref[W : 2 * W, at], v[0:W]], axis=0)
            a_ref[j, 0:W] = dot(q[0:W], kx, 1, 1)
            a_ref[j, W:] = dot(q[W:], k, 1, 1)
            b_ref[j, 0:W] = dot(g[0:W], vx, 1, 1)
            b_ref[j, W:] = dot(g[W:], v, 1, 1)
        rows = row_ref[pl.ds(i * WSTEP, WSTEP), :]
        cols = rows.T
        for j in range(WSTEP):
            row = rows[j : j + 1, :]
            shifted = jnp.concatenate([row[:, W:], row[:, :W]], axis=1)
            keys = jnp.concatenate([jnp.broadcast_to(shifted, (W, DH)), jnp.broadcast_to(row, (W, DH))], axis=0)
            a, b = a_ref[j], b_ref[j]
            decay = jnp.exp(cols[:, j : j + 1] - keys + lin_ref[...])
            logits = a * scale + win_ref[...]
            e = jnp.exp(logits - jnp.max(logits, axis=1, keepdims=True))
            inv = 1.0 / jnp.sum(e, axis=1, keepdims=True)
            delta = jnp.sum(e * b, axis=1, keepdims=True) * inv
            w1_ref[j] = (e * inv + decay * a).astype(BF16)
            w2_ref[j] = (e * (inv * scale) * (b - delta) + decay * b).astype(BF16)
        for j, at in enumerate(heads):
            q, k, v, g = q_ref[:, at], k_ref[:, at], v_ref[:, at], g_ref[:, at]
            kx = jnp.concatenate([halo_ref[0:W, at], k[0:W]], axis=0)
            vx = jnp.concatenate([halo_ref[W : 2 * W, at], v[0:W]], axis=0)
            w1, w2 = w1_ref[j], w2_ref[j]
            o_ref[0:W, at] = (dot(w1[0:W], vx, 1, 0)).astype(BF16)
            o_ref[W:, at] = (dot(w1[W:], v, 1, 0)).astype(BF16)
            qg_ref[0:W, at] = (dot(w2[0:W], kx, 1, 0)).astype(BF16)
            qg_ref[W:, at] = (dot(w2[W:], k, 1, 0)).astype(BF16)
            k_top = dot(w2[0:W], q[0:W], 0, 0)
            k_low = dot(w2[W:], q[W:], 0, 0)
            v_top = dot(w1[0:W], g[0:W], 0, 0)
            v_low = dot(w1[W:], g[W:], 0, 0)
            kg_ref[0:W, at] = (k_low[0:W] + k_top[W:]).astype(BF16)
            kg_ref[W:, at] = (k_low[W:]).astype(BF16)
            vg_ref[0:W, at] = (v_low[0:W] + v_top[W:]).astype(BF16)
            vg_ref[W:, at] = (v_low[W:]).astype(BF16)
            back_ref[0:W, at] = k_top[0:W].astype(BF16)
            back_ref[W : 2 * W, at] = v_top[0:W].astype(BF16)
            if j % 2 == 1:
                for copy in out_copies(i * (WSTEP // 2) + j // 2):
                    copy.start()
        return carry

    lax.fori_loop(0, 16 // WSTEP, step, 0)
    if WSTEP < 16:
        kept.start()
    for i in range(8):
        for copy in out_copies(i):
            copy.wait()
    kept.wait()


def final_kernel(lin_scale, n_alias, sel_ref, inputs_ref, ret_ref, row_ref, st_ref, parts_ref, *rest):
    outs = rest[n_alias : n_alias + 4]
    stage_ref, sems = rest[n_alias + 4 :]
    q_ref, k_ref, v_ref, g_ref = (inputs_ref.at[n] for n in range(4))
    po_ref, pq_ref, pk_ref, pv_ref = (parts_ref.at[n] for n in range(4))
    sel = sel_ref[0]
    rows = row_ref[pl.ds(pl.multiple_of(sel * HALF, HALF), HALF), :]
    heads = jnp.exp(rows).T * lin_scale
    tails = jnp.exp(rows[:, DH - 1 :] - rows).T * lin_scale
    width = OSTEP * DH
    copies = []

    def send(n, j):
        if j % OSTEP == OSTEP - 1:
            i = j // OSTEP
            target = pl.ds(pl.multiple_of(sel * COLS + i * width, width), width)
            copy = pltpu.make_async_copy(stage_ref.at[n, :, i * width : (i + 1) * width], outs[n].at[:, target], sems.at[i, n])
            copy.start()
            copies.append(copy)

    for j in range(HALF):
        at = pl.ds(pl.multiple_of(sel * COLS + j * DH, DH), DH)
        to = slice(j * DH, (j + 1) * DH)
        head = heads[:, j : j + 1]
        s = jnp.concatenate([st_ref[2 * j, 0:64, :], st_ref[2 * j + 1, 0:64, :]], axis=0)
        stage_ref[0, :, to] = (po_ref[:, at].astype(F32) + head * dot(q_ref[:, at], s, 1, 0)).astype(BF16)
        stage_ref[1, :, to] = (pq_ref[:, at].astype(F32) + head * dot(g_ref[:, at], s, 1, 1)).astype(BF16)
        send(0, j)
        send(1, j)
    for j in range(HALF):
        at = pl.ds(pl.multiple_of(sel * COLS + j * DH, DH), DH)
        to = slice(j * DH, (j + 1) * DH)
        tail = tails[:, j : j + 1]
        m = jnp.concatenate([st_ref[2 * j, 64:128, :], st_ref[2 * j + 1, 64:128, :]], axis=0)
        kg = pk_ref[:, at].astype(F32) + tail * dot(v_ref[:, at], m, 1, 1)
        vg = pv_ref[:, at].astype(F32) + tail * dot(k_ref[:, at], m, 1, 0)
        stage_ref[2, 0:W, to] = kg[0:W].astype(BF16)
        stage_ref[2, W:, to] = (kg[W:] + ret_ref[0:W, at].astype(F32)).astype(BF16)
        stage_ref[3, 0:W, to] = vg[0:W].astype(BF16)
        stage_ref[3, W:, to] = (vg[W:] + ret_ref[W : 2 * W, at].astype(F32)).astype(BF16)
        send(2, j)
        send(3, j)
    for copy in copies:
        copy.wait()


def vmem(mib):
    return pltpu.CompilerParams(vmem_limit_bytes=mib << 20)


def cost(flops, nbytes):
    return pl.CostEstimate(flops=int(flops), bytes_accessed=int(nbytes), transcendentals=0)


IN_VMEM = pl.BlockSpec(memory_space=pltpu.VMEM)
IN_HBM = pl.BlockSpec(memory_space=pltpu.HBM)
IN_SMEM = pl.BlockSpec(memory_space=pltpu.SMEM)
DMA = pltpu.SemaphoreType.DMA


def local_states(sel, q, k, v, g, gates, with_halo):
    outs = [pltpu.VMEM((PLANE, MSG, DH), BF16)]
    sems = [DMA((HALF // STEP, 4)), DMA]
    if with_halo:
        outs.append(pltpu.VMEM((2 * W, 2048), BF16))
        sems.append(DMA((2,)))
    return pl.pallas_call(
        lambda *refs: states_kernel(with_halo, *refs),
        out_shape=tuple(outs),
        in_specs=[IN_SMEM] + [IN_HBM] * 5,
        out_specs=(IN_VMEM,) * len(outs),
        scratch_shapes=[pltpu.VMEM((128, COLS), BF16)] * 4 + [pltpu.VMEM((HALF, DH), F32)] + sems,
        cost_estimate=cost(7e7, 1.6e6),
        compiler_params=vmem(8),
        name="local_states",
    )(sel, q, k, v, g, gates)


def small_call(body, scalar, arrays, outs):
    return pl.pallas_call(
        body,
        out_shape=tuple(pltpu.VMEM(s, BF16) for s in outs),
        in_specs=[IN_SMEM] + [IN_VMEM] * len(arrays),
        out_specs=(IN_VMEM,) * len(outs),
        cost_estimate=cost(1e6, 2e6),
        compiler_params=vmem(4),
    )(scalar, *arrays)


def window(lin_scale, live, q, k, v, g, halo, gates):
    full = (128, 2048)
    steps = 16 // WSTEP
    return pl.pallas_call(
        lambda *refs: window_kernel(lin_scale, *refs),
        out_shape=(pltpu.HBM((4, *full), BF16), pltpu.HBM((4, *full), BF16), pltpu.HBM(full, BF16), pltpu.VMEM((16, DH), F32)),
        in_specs=[IN_SMEM] + [IN_HBM] * 4 + [IN_VMEM, IN_HBM],
        out_specs=(IN_HBM,) * 3 + (IN_VMEM,),
        scratch_shapes=[pltpu.VMEM((4, *full), BF16), pltpu.VMEM((4, *full), BF16), pltpu.VMEM(full, BF16)]
        + [pltpu.VMEM((WSTEP, DH, DH), t) for t in (F32, F32, BF16, BF16)]
        + [pltpu.VMEM((DH, DH), F32)] * 2
        + [pltpu.VMEM((16, DH), F32), DMA((steps, 4)), DMA((8, 2)), DMA, DMA],
        cost_estimate=cost(6e8, 8e6),
        compiler_params=vmem(14),
        name="window",
    )(live, q, k, v, g, halo, gates)


def finish(lin_scale, sel, inputs, ret, rows, states, parts, previous):
    n = len(previous)
    return pl.pallas_call(
        lambda *refs: final_kernel(lin_scale, n, *refs),
        out_shape=tuple(pltpu.HBM((128, 2048), BF16) for _ in range(4)),
        in_specs=[IN_SMEM] + [IN_VMEM] * 5 + [IN_HBM] * n,
        out_specs=(IN_HBM,) * 4,
        scratch_shapes=[pltpu.VMEM((4, 128, COLS), BF16), DMA((HALF // OSTEP, 4))],
        input_output_aliases={6 + i: i for i in range(n)},
        cost_estimate=cost(3e8, 5e6),
        compiler_params=vmem(8),
        name="finish",
    )(sel, inputs, ret, rows, states, parts, *previous)


def per_device(q, k, v, g, gates):
    lin_scale = (DH * q.shape[0] * 256) ** (-0.5)
    core = lax.axis_index("c")
    mine = core[None].astype(jnp.int32)
    theirs = 1 - mine
    z = lax.axis_index("z")[None].astype(jnp.int32)
    live = (lax.axis_index(AXES) > 0)[None].astype(jnp.int32)
    swap = [(0, 1), (1, 0)]
    q, k, v, g, gates = (pltpu.with_memory_space_constraint(a, pltpu.HBM) for a in (q, k, v, g, gates))

    sent, edge = local_states(theirs, q, k, v, g, gates, True)
    other = lax.ppermute(sent, "c", swap)
    halo = lax.ppermute(edge, AXES, [(i, i + 1) for i in range(255)])
    (own,) = local_states(mine, q, k, v, g, gates, False)
    chip, other = small_call(combine_kernel, mine, (own, other), [(PLANE, MSG, DH)] * 2)
    plane = lax.all_to_all(chip, ("x", "y"), 0, 0, tiled=True)
    parts, inputs, back, sums = window(lin_scale, live, q, k, v, g, halo, gates)
    (total,) = small_call(plane_kernel, z, (plane,), [(GRID[0], 80, DH)])
    planes = lax.all_to_all(total, "z", 0, 0, tiled=True)
    ret = lax.ppermute(back, AXES, [(i + 1, i) for i in range(255)])
    (incoming,) = small_call(incoming_kernel, z, (plane, planes), [(PLANE, DH, DH)])
    chip_in = lax.all_to_all(incoming, ("x", "y"), 0, 0, tiled=True)
    st_mine, st_theirs = small_call(hand_kernel, mine, (chip_in, own, other), [(PLANE, DH, DH)] * 2)
    st_other = lax.ppermute(st_theirs, "c", swap)
    outs = finish(lin_scale, mine, inputs, ret, sums, st_mine, parts, ())
    return finish(lin_scale, theirs, inputs, ret, sums, st_other, parts, outs)


def solution(mesh):
    fine = Mesh(mesh.devices.reshape(GRID), AXES)
    rows = P(AXES, None)

    return jax.shard_map(
        per_device,
        mesh=fine,
        in_specs=(rows,) * 4 + (P(None, AXES),),
        out_specs=(rows,) * 4,
        check_vma=False,
    )
```
